128 devices in a mesh: dp: 32 (over z, y, core), graph: 4 (over x).
Axes of the slice: x: 4, y: 4, z: 4, core: 2. Of those that a mesh axis runs over, the one named last changes fastest.
Arguments:
- atoms: bfloat16 [32, 4, 1024, 128], P('dp', 'graph'), may hold values from -80 to 80, as said below
- gain: float32 [128], replicated, may hold values from 0.1 to 1.9
- w_src: bfloat16 [128, 128], replicated, may hold values from -0.5 to 0.5
- w_edge: bfloat16 [128, 128], replicated, may hold values from -0.5 to 0.5
- w_out: bfloat16 [128, 128], replicated, may hold values from -0.5 to 0.5
- send_src: int32 [32, 4, 4, 2048], P('dp', 'graph'), may hold values from 0 to 1023
- recv_dst: int32 [32, 4, 4, 2048], P('dp', 'graph'), may hold values from 0 to 1023
- edge_count: int32 [32, 4, 4], P('dp'), may hold values from 512 to 2048, as said below
- edge_feat: bfloat16 [32, 4, 4, 2048, 128], P('dp', 'graph'), may hold values from -6 to 6
- cotangent: bfloat16 [32, 4, 1024, 128], P('dp', 'graph'), may hold values from -6 to 6
Outputs:
- layer_out: bfloat16 [32, 4, 1024, 128], P('dp', 'graph')
- grad_atoms: bfloat16 [32, 4, 1024, 128], P('dp', 'graph')
- grad_w_src: float32 [128, 128], P('dp')
- grad_w_edge: float32 [128, 128], P('dp')
- grad_w_out: float32 [128, 128], P('dp')
- grad_gain: float32 [128], P('dp')
The draws below stay inside these ranges and needn't reach their ends.
Inputs may be any that keep to these rules, and one draw needn't show every extreme that they name: `atoms`: row scales of the atom features vary. `edge_count`: every batch has one destination shard that receives more; in every draw some shard sends exactly 2048 live slots to some shard.
All inputs are finite; a program needn't handle non-finite values.
Results may differ from the reference program's by a relative error of at most 0.0059.
Values may be sent and summed in bfloat16 or wider, within the bound.
A program may use at most 64 MiB of HBM per device.

```python
import math
import jax
import jax.numpy as jnp
from jax import lax

C = 128
H = 128
EDGE = 128
A_DEV = 1024
CAP = 2048
DEG_NORM = 23
N_DP = 32
N_GRAPH = 4


def draw_atoms(key, part):
    first, second = jax.random.split(jax.random.fold_in(key, 5), 2)
    shape = (N_DP, N_GRAPH, A_DEV, C)
    base = jax.random.normal(first, shape, jnp.float32)
    scales = jnp.exp(jax.random.uniform(second, (N_DP, N_GRAPH, A_DEV, 1), jnp.float32, 0.0, math.log(10.0)))
    values = base * scales
    return jnp.clip(values, -80.0, 80.0).astype(jnp.bfloat16)


def draw_edge_count(key, part):
    keys = jax.random.split(jax.random.fold_in(key, 3), 5)
    base = jax.random.randint(keys[0], (N_DP, N_GRAPH, N_GRAPH), CAP // 4, CAP // 2 + 1)
    hot = jax.random.randint(keys[1], (N_DP, 1, 1), 0, N_GRAPH)
    extra = jax.random.randint(keys[2], (N_DP, N_GRAPH, N_GRAPH), 0, CAP // 2)
    target = jnp.arange(N_GRAPH, dtype=jnp.int32)[None, None, :]
    counts = base + jnp.where(target == hot, extra, 0)
    row_pick = jax.random.randint(keys[3], (), 0, N_GRAPH)
    col_pick = jax.random.randint(keys[4], (), 0, N_GRAPH)
    counts = counts.at[:, row_pick, col_pick].set(CAP)
    return counts.astype(jnp.int32)


def place_ends(entries, own_key, least, top_value):
    place = [jax.random.randint(jax.random.fold_in(own_key, axis), (), 0, length) for axis, length in enumerate(entries.shape)]
    longest = entries.shape.index(max(entries.shape))
    next_to = place[:longest] + [(place[longest] + 1) % entries.shape[longest]] + place[longest + 1:]
    return entries.at[tuple(place)].set(least).at[tuple(next_to)].set(top_value)


def steps_of(key, shape, cuts, least, largest):
    def one(position, shards_of):
        heights = jax.random.uniform(jax.random.fold_in(jax.random.fold_in(key, 6), position), (shards_of,), jnp.float32, least / len(cuts), largest / len(cuts))
        return jnp.repeat(jnp.exp(heights), shape[position] // shards_of).reshape((-1,) + (1,) * (len(shape) - position - 1))

    loudness = one(*cuts[0])
    for cut in cuts[1:]:
        loudness = loudness * one(*cut)
    return loudness


def noise(key, shape, scale, bound, pieces=(), kind=jnp.bfloat16):
    values = scale * jax.random.normal(key, shape, jnp.float32)
    if pieces:
        values = values * steps_of(key, shape, pieces, -0.22, 0.18)
    return jnp.clip(values, -bound, bound).astype(kind)


def setup_inputs(seed: int = 0) -> dict:
    arg_keys = jax.random.split(jax.random.key(seed), 11)
    return {
        "atoms": draw_atoms(jax.random.fold_in(arg_keys[10], 71), 0),
        "gain": jnp.clip(1.0 + 0.18 * jax.random.normal(arg_keys[1], (C,), jnp.float32), 0.1, 1.9),
        "w_src": noise(arg_keys[2], (C, H), C ** -0.5, 0.5),
        "w_edge": noise(arg_keys[3], (EDGE, H), EDGE ** -0.5, 0.5),
        "w_out": noise(arg_keys[4], (H, C), H ** -0.5, 0.5),
        "send_src": place_ends(jax.random.randint(arg_keys[5], (N_DP, N_GRAPH, N_GRAPH, CAP), 0, A_DEV), jax.random.fold_in(arg_keys[5], 1), 0, A_DEV - 1).astype(jnp.int32),
        "recv_dst": place_ends(jax.random.randint(arg_keys[6], (N_DP, N_GRAPH, N_GRAPH, CAP), 0, A_DEV), jax.random.fold_in(arg_keys[6], 1), 0, A_DEV - 1).astype(jnp.int32),
        "edge_count": draw_edge_count(jax.random.fold_in(arg_keys[10], 71), 0),
        "edge_feat": noise(arg_keys[8], (N_DP, N_GRAPH, N_GRAPH, CAP, EDGE), 1.0, 6.0, ((0, 32), (1, 4))),
        "cotangent": noise(arg_keys[9], (N_DP, N_GRAPH, A_DEV, C), 1.0, 6.0, ((0, 32), (1, 4))),
    }


def silu_slope(pre):
    sig = jax.nn.sigmoid(pre)
    return sig * (1.0 + pre * (1.0 - sig))

def reference(atoms, gain, w_src, w_edge, w_out, send_src, recv_dst, edge_count, edge_feat, cotangent):

    def one_batch(inputs):
        feats, srcs, dsts, counts, edges, cot = inputs
        hfull = feats.astype(jnp.float32)
        inv = lax.rsqrt(lax.optimization_barrier(jnp.mean(hfull * hfull, axis=-1)) + 1e-06)
        normed = (hfull * inv[..., None] * gain).astype(jnp.bfloat16).reshape(N_GRAPH * A_DEV, C)
        src_flat = (jnp.arange(N_GRAPH, dtype=jnp.int32)[:, None, None] * A_DEV + srcs).reshape(-1)
        rows = jnp.take(normed, src_flat, axis=0)
        edge_rows = edges.reshape(-1, EDGE)
        pre = jnp.dot(rows, w_src, preferred_element_type=jnp.float32) + jnp.dot(edge_rows, w_edge, preferred_element_type=jnp.float32)
        valid = (jnp.arange(CAP, dtype=jnp.int32)[None, None, :] < counts[:, :, None]).astype(jnp.float32).reshape(-1, 1)
        msg = (jax.nn.silu(pre) * valid).astype(jnp.bfloat16)
        dst_local = jnp.transpose(dsts, (1, 0, 2))
        dst_flat = (jnp.arange(N_GRAPH, dtype=jnp.int32)[None, :, None] * A_DEV + dst_local).reshape(-1)
        agg = (jax.ops.segment_sum(msg.astype(jnp.float32), dst_flat, num_segments=N_GRAPH * A_DEV) / DEG_NORM).astype(jnp.bfloat16)
        out = (hfull.reshape(-1, C) + jnp.dot(agg, w_out, preferred_element_type=jnp.float32)).astype(jnp.bfloat16)
        cot_flat = cot.reshape(-1, C)
        back = (lax.dot_general(cot_flat, w_out, (((1,), (1,)), ((), ())), preferred_element_type=jnp.float32) / DEG_NORM).astype(jnp.bfloat16)
        slot_back = jnp.take(back, dst_flat, axis=0)
        dpre = (slot_back.astype(jnp.float32) * silu_slope(pre) * valid).astype(jnp.bfloat16)
        grad_src = lax.dot_general(rows, dpre, (((0,), (0,)), ((), ())), preferred_element_type=jnp.float32)
        grad_edge = lax.dot_general(edge_rows, dpre, (((0,), (0,)), ((), ())), preferred_element_type=jnp.float32)
        grad_out = lax.dot_general(agg, cot_flat, (((0,), (0,)), ((), ())), preferred_element_type=jnp.float32)
        dnorm_rows = lax.dot_general(dpre, w_src, (((1,), (1,)), ((), ())), preferred_element_type=jnp.float32)
        dnorm = jax.ops.segment_sum(dnorm_rows, src_flat, num_segments=N_GRAPH * A_DEV).reshape(N_GRAPH, A_DEV, C)
        scaled = gain * dnorm
        grad_g = lax.optimization_barrier(jnp.sum(dnorm * hfull * inv[..., None], axis=(0, 1)))
        grad_h = cot.astype(jnp.float32) + inv[..., None] * scaled - hfull * (inv ** 3)[..., None] * lax.optimization_barrier(jnp.mean(hfull * scaled, axis=-1, keepdims=True))
        return (out.reshape(N_GRAPH, A_DEV, C), grad_h.astype(jnp.bfloat16), grad_src, grad_edge, grad_out, grad_g)
    outs = lax.map(one_batch, (atoms, send_src, recv_dst, edge_count, edge_feat, cotangent))
    layer_out, grad_atoms, grad_src, grad_edge, grad_out, grad_g = outs
    return (layer_out, grad_atoms, lax.optimization_barrier(jnp.sum(grad_src, axis=0)), lax.optimization_barrier(jnp.sum(grad_edge, axis=0)), lax.optimization_barrier(jnp.sum(grad_out, axis=0)), lax.optimization_barrier(jnp.sum(grad_g, axis=0)))
```

```python
import functools

import jax
import jax.numpy as jnp
from jax import lax
from jax.experimental import pallas as pl
from jax.experimental.pallas import tpu as pltpu
from jax.sharding import PartitionSpec as P

DEG_NORM = 23.0
TILE = 1024
MESH = pl.DeviceIdType.MESH
F32 = jnp.float32
BF16 = jnp.bfloat16
VMEM_LIMIT = 56 << 20


def mm(a, b, ca, cb):
    return lax.dot_general(a, b, (((ca,), (cb,)), ((), ())), preferred_element_type=F32)


def split(x):
    hi = x.astype(BF16)
    return hi, (x - hi.astype(F32)).astype(BF16)


def one_hot(index, atoms):
    rows = lax.broadcasted_iota(jnp.int32, (atoms, index.shape[1]), 0)
    return (rows == index).astype(F32).astype(BF16)


def norm_parts(h):
    return lax.rsqrt(jnp.mean(h * h, axis=-1, keepdims=True) + 1e-06)


def forward_kernel(shards, counts, atoms, gain, w_src, w_edge, src, dst0, dst1, dst2, dst3, feat, own, out1, out2, out3, slope, normed_t):
    me = lax.axis_index("graph")
    atom_count = atoms.shape[0]
    h = atoms[...].astype(F32)
    normed = (h * norm_parts(h) * gain[...]).astype(BF16)
    normed_t[...] = normed.T
    dsts = (dst0, dst1, dst2, dst3)
    outs = (own, out1, out2, out3)
    w_src_t = w_src[...].T
    w_edge_t = w_edge[...].T
    for j in range(shards):
        peer = lax.rem(me + j, shards)
        live = counts[me, peer]

        def contribution(t):
            span = pl.ds(t * TILE, TILE)
            rows_t = mm(normed_t[...], one_hot(src[pl.ds(peer, 1), span], atom_count), 1, 0).astype(BF16)
            pre = mm(w_src_t, rows_t, 1, 0) + mm(w_edge_t, feat[peer, span, :], 1, 1)
            sig = 0.5 * jnp.tanh(0.5 * pre) + 0.5
            slot = t * TILE + lax.broadcasted_iota(jnp.int32, pre.shape, 1)
            sig = jnp.where(slot < live, sig, 0.0)
            msg = (pre * sig).astype(BF16)
            slope[j, :, span] = (sig * (1.0 + pre * (1.0 - sig))).astype(BF16)
            return mm(one_hot(dsts[j][pl.ds(me, 1), span], atom_count), msg, 1, 1)

        first = contribution(0)

        @pl.when(live <= TILE)
        def _():
            outs[j][...] = first.astype(outs[j].dtype)

        @pl.when(live > TILE)
        def _():
            outs[j][...] = (first + contribution(1)).astype(outs[j].dtype)


def backward_kernel(shards, counts, atoms, gain, w_src, w_out, src, dst0, dst1, dst2, dst3, cot0, cot1, cot2, cot3, feat, slope,
                    grad_atoms, grad_src, grad_edge, grad_gain, back, acc, edge_t):
    me = lax.axis_index("graph")
    atom_count = atoms.shape[0]
    dsts = (dst0, dst1, dst2, dst3)
    cots = (cot0, cot1, cot2, cot3)
    for j in range(shards):
        peer = lax.rem(me + j, shards)
        live = counts[me, peer]
        back[...] = (mm(w_out[...], cots[j][...], 1, 1) / DEG_NORM).astype(BF16)

        def contribution(t):
            span = pl.ds(t * TILE, TILE)
            slot_back = mm(back[...], one_hot(dsts[j][pl.ds(me, 1), span], atom_count), 1, 0)
            dpre = (slot_back * slope[j, :, span].astype(F32)).astype(BF16)
            edge = mm(dpre, feat[peer, span, :], 1, 0)
            return edge, mm(one_hot(src[pl.ds(peer, 1), span], atom_count), dpre, 1, 1)

        edge, total = contribution(0)
        if j == 0:
            edge_t[...] = edge
            acc[...] = total
        else:
            edge_t[...] += edge
            acc[...] += total

        @pl.when(live > TILE)
        def _():
            edge, total = contribution(1)
            edge_t[...] += edge
            acc[...] += total

    h = atoms[...].astype(F32)
    inv = norm_parts(h)
    normed = (h * inv * gain[...]).astype(BF16)
    hi, lo = split(acc[...])
    weight = w_src[...]
    dnorm = mm(hi, weight, 1, 1) + mm(lo, weight, 1, 1)
    grad_src[...] = mm(normed, hi, 0, 0) + mm(normed, lo, 0, 0)
    grad_edge[...] = edge_t[...].T
    scaled = gain[...] * dnorm
    grad_gain[...] = jnp.sum(dnorm * h * inv, axis=0, keepdims=True)
    grad_atoms[...] = (
        cots[0][...].astype(F32)
        + inv * scaled
        - h * (inv * inv * inv) * jnp.mean(h * scaled, axis=-1, keepdims=True)
    ).astype(BF16)


def output_kernel(pieces, atoms, cot, w_out, own, in1, in2, in3, grad_src, grad_edge, grad_gain, layer_out, packed, grad_out):
    summed = own[...] + in1[...].astype(F32) + in2[...].astype(F32) + in3[...].astype(F32)
    agg = (summed / DEG_NORM).astype(BF16)
    layer_out[...] = (atoms[...].astype(F32) + mm(agg, w_out[...], 1, 0)).astype(BF16)
    grad_out[...] = mm(agg, cot[...], 0, 0)
    rows = grad_src.shape[0] // pieces
    for i in range(pieces):
        span = pl.ds(i * rows, rows)
        packed[i, 0:rows, :] = grad_src[span, :]
        packed[i, rows:2 * rows, :] = grad_edge[span, :]
        packed[i, 2 * rows:3 * rows, :] = grad_out[span, :]
        packed[i, 3 * rows:4 * rows, :] = jnp.broadcast_to(grad_gain[...], (rows, grad_gain.shape[1]))


def reduce_kernel(pieces, shards, packed, out_src, out_edge, out_out, out_gain, landed, held, send1, recv1, send2, recv2):
    dp = lax.axis_index("dp")
    graph = lax.axis_index("graph")
    barrier = pltpu.get_barrier_semaphore()
    for k in range(1, pieces):
        pl.semaphore_signal(barrier, inc=1, device_id=(lax.rem(dp + k, pieces), graph), device_id_type=MESH)
    for k in range(1, shards):
        pl.semaphore_signal(barrier, inc=1, device_id=(dp, lax.rem(graph + k, shards)), device_id_type=MESH)
    pl.semaphore_wait(barrier, pieces + shards - 2)
    copies = []
    for k in range(1, pieces):
        target = lax.rem(dp + k, pieces)
        copies.append(pltpu.make_async_remote_copy(
            src_ref=packed.at[target], dst_ref=landed.at[k - 1], send_sem=send1.at[k - 1], recv_sem=recv1.at[k - 1],
            device_id=(target, graph), device_id_type=MESH))
        copies[-1].start()
    for copy in copies:
        copy.wait_recv()
    total = packed[dp]
    for k in range(1, pieces):
        total = total + landed[k - 1]
    held[graph] = total
    swaps = []
    for k in range(1, shards):
        swaps.append(pltpu.make_async_remote_copy(
            src_ref=held.at[graph], dst_ref=held.at[graph], send_sem=send2.at[k - 1], recv_sem=recv2.at[k - 1],
            device_id=(dp, lax.rem(graph + k, shards)), device_id_type=MESH))
        swaps[-1].start()
    for copy in copies:
        copy.wait_send()
    for copy in swaps:
        copy.wait()
    total = held[0]
    for k in range(1, shards):
        total = total + held[k]
    rows = out_src.shape[0]
    out_src[...] = total[0:rows, :]
    out_edge[...] = total[rows:2 * rows, :]
    out_out[...] = total[2 * rows:3 * rows, :]
    lanes = total.shape[1]
    gains = jnp.broadcast_to(total[3 * rows:3 * rows + 1, :], (8, lanes))
    out_gain[...] = pltpu.roll(gains, lax.rem(lanes - dp * rows, lanes), 1)[0:1, 0:rows]


def body(dp, shards, atoms, gain, w_src, w_edge, w_out, send_src, recv_dst, edge_count, edge_feat, cotangent):
    atom_count, chans = atoms.shape[2:]
    slots = send_src.shape[3]
    width = w_src.shape[1]
    vmem = pl.BlockSpec(memory_space=pltpu.VMEM)
    smem = pl.BlockSpec(memory_space=pltpu.SMEM)
    shape = jax.ShapeDtypeStruct

    def from_peer(x, j):
        return lax.ppermute(x, "graph", [((i + j) % shards, i) for i in range(shards)])

    def to_peer(x, j):
        return lax.ppermute(x, "graph", [(i, (i + j) % shards) for i in range(shards)])

    params = pltpu.CompilerParams(vmem_limit_bytes=VMEM_LIMIT)
    atoms2 = atoms.reshape(atom_count, chans)
    gain2 = gain.reshape(1, chans)
    src2 = send_src.reshape(shards, slots)
    dst2 = recv_dst.reshape(shards, slots)
    cot2 = cotangent.reshape(atom_count, chans)
    feat = edge_feat.reshape(shards, slots, edge_feat.shape[4])
    counts = edge_count.reshape(shards, shards)
    dsts = [dst2] + [from_peer(dst2, j) for j in range(1, shards)]
    cots = [cot2] + [from_peer(cot2, j) for j in range(1, shards)]
    own, *parts, slope = pl.pallas_call(
        functools.partial(forward_kernel, shards),
        out_shape=[shape((atom_count, width), F32)] + [shape((atom_count, width), BF16)] * (shards - 1)
        + [shape((shards, width, slots), BF16)],
        in_specs=[smem] + [vmem] * (6 + shards),
        out_specs=[vmem] * (shards + 1),
        scratch_shapes=[pltpu.VMEM((chans, atom_count), BF16)],
        compiler_params=params,
        cost_estimate=pl.CostEstimate(flops=12_000_000_000, bytes_accessed=8_000_000, transcendentals=1_000_000),
        name="forward",
    )(counts, atoms2, gain2, w_src, w_edge, src2, *dsts, feat)
    arrived = [to_peer(parts[j - 1], j) for j in range(1, shards)]
    grad_atoms, grad_src, grad_edge, grad_gain = pl.pallas_call(
        functools.partial(backward_kernel, shards),
        out_shape=[shape((atom_count, chans), BF16), shape((chans, width), F32), shape((chans, width), F32), shape((1, chans), F32)],
        in_specs=[smem] + [vmem] * (7 + 2 * shards),
        out_specs=[vmem] * 4,
        scratch_shapes=[pltpu.VMEM((width, atom_count), BF16), pltpu.VMEM((atom_count, width), F32), pltpu.VMEM((width, chans), F32)],
        compiler_params=params,
        cost_estimate=pl.CostEstimate(flops=12_000_000_000, bytes_accessed=8_000_000, transcendentals=0),
        name="backward",
    )(counts, atoms2, gain2, w_src, w_out, src2, *dsts, *cots, feat, slope)
    rows = chans // dp
    layer_out, packed = pl.pallas_call(
        functools.partial(output_kernel, dp),
        out_shape=[shape((atom_count, chans), BF16), shape((dp, 4 * rows, chans), F32)],
        in_specs=[vmem] * 10,
        out_specs=[vmem] * 2,
        scratch_shapes=[pltpu.VMEM((width, chans), F32)],
        compiler_params=params,
        name="output",
    )(atoms2, cot2, w_out, own, *arrived, grad_src, grad_edge, grad_gain)
    piece = (4 * rows, chans)
    out_src, out_edge, out_out, out_gain = pl.pallas_call(
        functools.partial(reduce_kernel, dp, shards),
        out_shape=[shape((rows, width), F32)] * 3 + [shape((1, rows), F32)],
        in_specs=[vmem],
        out_specs=[vmem] * 4,
        scratch_shapes=[
            pltpu.VMEM((dp - 1,) + piece, F32),
            pltpu.VMEM((shards,) + piece, F32),
            pltpu.SemaphoreType.DMA((dp - 1,)),
            pltpu.SemaphoreType.DMA((dp - 1,)),
            pltpu.SemaphoreType.DMA((shards - 1,)),
            pltpu.SemaphoreType.DMA((shards - 1,)),
        ],
        compiler_params=pltpu.CompilerParams(collective_id=0, has_side_effects=True),
        name="reduce",
    )(packed)
    return (layer_out.reshape(atoms.shape), grad_atoms.reshape(atoms.shape), out_src, out_edge, out_out, out_gain.reshape(rows))


def solution(mesh):
    in_specs = (
        P("dp", "graph", None, None),
        P(),
        P(),
        P(),
        P(),
        P("dp", "graph", None, None),
        P("dp", "graph", None, None),
        P("dp", None, None),
        P("dp", "graph", None, None, None),
        P("dp", "graph", None, None),
    )
    out_specs = (
        P("dp", "graph", None, None),
        P("dp", "graph", None, None),
        P("dp", None),
        P("dp", None),
        P("dp", None),
        P("dp"),
    )
    return jax.shard_map(
        functools.partial(body, mesh.shape["dp"], mesh.shape["graph"]),
        mesh=mesh, in_specs=in_specs, out_specs=out_specs, check_vma=False)
```

```python
import functools

import jax
import jax.numpy as jnp
from jax import lax
from jax.experimental import pallas as pl
from jax.experimental.pallas import tpu as pltpu
from jax.sharding import PartitionSpec as P

DEG_NORM = 23.0
TILE = 1024
LANES = 128
MESH = pl.DeviceIdType.MESH
F32 = jnp.float32
BF16 = jnp.bfloat16
I16 = jnp.int16
VMEM_LIMIT = 56 << 20


def mm(a, b, ca, cb):
    return lax.dot_general(a, b, (((ca,), (cb,)), ((), ())), preferred_element_type=F32)


def split(x):
    hi = x.astype(BF16)
    return hi, (x - hi.astype(F32)).astype(BF16)


def ones_where(mask):
    return jnp.where(mask, jnp.array(1, BF16), jnp.array(0, BF16))


def pick_form(index, atoms):
    rows = lax.broadcasted_iota(jnp.int32, (atoms, index.shape[1]), 0).astype(I16)
    return ones_where(rows == index.astype(I16))


def sum_form(index, atoms):
    column = jnp.concatenate([
        jnp.broadcast_to(index[:, k:k + LANES], (LANES, LANES)).astype(F32).T.astype(jnp.int32).astype(I16)
        for k in range(0, index.shape[1], LANES)
    ], 0)
    return jnp.concatenate([
        ones_where((lax.broadcasted_iota(jnp.int32, column.shape, 1) + a).astype(I16) == column)
        for a in range(0, atoms, LANES)
    ], 1)


def layer_kernel(pieces, counts, atoms, gain, w_src, w_edge, w_out, src, dst, cot, feat_hbm,
                 layer_out, grad_atoms, sums,
                 dst_in, cot_in, feat, msg, slope, partial, far_out, far_in, near_out, near_in, acc,
                 pack_a, pack_b, land_a, land_b, held,
                 feat_sem, dst_send, dst_recv, cot_send, cot_recv, part_send, part_recv,
                 a_send, a_recv, b_send, b_recv, s_send, s_recv):
    dp = lax.axis_index("dp")
    me = lax.axis_index("graph")
    shards = 4
    atom_count, chans = atoms.shape
    slots = src.shape[1]
    half_atoms, half_rows = atom_count // 2, acc.shape[0] // 2
    right, left = lax.rem(me + 1, shards), lax.rem(me + shards - 1, shards)

    barrier = pltpu.get_barrier_semaphore()
    for k in range(1, shards):
        pl.semaphore_signal(barrier, inc=1, device_id=(dp, lax.rem(me + k, shards)), device_id_type=MESH)
    for k in range(1, pieces):
        pl.semaphore_signal(barrier, inc=1, device_id=(lax.rem(dp + k, pieces), me), device_id_type=MESH)

    def send(source, target, send_sem, recv_sem, device):
        copy = pltpu.make_async_remote_copy(
            src_ref=source, dst_ref=target, send_sem=send_sem, recv_sem=recv_sem, device_id=device, device_id_type=MESH)
        copy.start()
        return copy

    peers = [lax.rem(me + j, shards) for j in range(shards)]
    loads = [pltpu.make_async_copy(feat_hbm.at[peers[j]], feat.at[j], feat_sem.at[j]) for j in range(shards)]
    for j in (0, 2, 1, 3):
        loads[j].start()

    h = atoms[...].astype(F32)
    inv = lax.rsqrt(jnp.mean(h * h, axis=-1, keepdims=True) + 1e-06)
    normed_t = (h * inv * gain[...]).astype(BF16).T
    w_src_t = w_src[...].T
    w_edge_t = w_edge[...].T
    spans = [pl.ds(t, TILE) for t in range(0, slots, TILE)]

    def forward(j):
        loads[j].wait()
        for t, span in enumerate(spans):
            rows_t = mm(normed_t, pick_form(src[pl.ds(peers[j], 1), span], atom_count), 1, 0).astype(BF16)
            pre = mm(w_src_t, rows_t, 1, 0) + mm(w_edge_t, feat[j, span, :], 1, 1)
            sig = 0.5 * jnp.tanh(0.5 * pre) + 0.5
            slot = t * TILE + lax.broadcasted_iota(jnp.int32, pre.shape, 1)
            sig = jnp.where(slot < counts[me, peers[j]], sig, 0.0)
            msg[j, :, span] = (pre * sig).astype(BF16)
            slope[j, :, span] = sig * (1.0 + pre * (1.0 - sig))

    def targets(j, span):
        return dst[pl.ds(me, 1), span] if j == 0 else dst_in[j - 1, pl.ds(me, 1), span]

    def sum_messages(j):
        total = None
        for span in spans:
            part = mm(msg[j, :, span], sum_form(targets(j, span), atom_count), 1, 0)
            total = part if total is None else total + part
        return total

    def backward(j, cot_j, first):
        back = (mm(w_out[...], cot_j, 1, 1) / DEG_NORM).astype(BF16)
        edge, total = None, None
        for span in spans:
            slot_back = mm(back, pick_form(targets(j, span), atom_count), 1, 0)
            dpre = (slot_back * slope[j, :, span]).astype(BF16)
            e = mm(dpre, feat[j, span, :], 1, 0)
            a = mm(dpre, sum_form(src[pl.ds(peers[j], 1), span], atom_count), 1, 0)
            edge = e if edge is None else edge + e
            total = a if total is None else total + a
        acc[...] = total if first else acc[...] + total
        return edge

    forward(0)
    pl.semaphore_wait(barrier, pieces + shards - 2)
    dst_copies = []
    for k in (2, 1, 3):
        dst_copies.append(send(dst, dst_in.at[shards - k - 1], dst_send.at[shards - k - 1], dst_recv.at[shards - k - 1], (dp, peers[k])))
    cot_left = send(cot, cot_in.at[0], cot_send.at[0], cot_recv.at[0], (dp, left))
    cot_right = send(cot, cot_in.at[2], cot_send.at[1], cot_recv.at[1], (dp, right))
    for j in (2, 1, 3):
        forward(j)
    for copy in dst_copies:
        copy.wait_recv()

    far_out[...] = sum_messages(2).astype(BF16)
    first_half, second_half = pl.ds(0, half_rows), pl.ds(half_rows, half_rows)
    far_right = send(far_out.at[first_half], far_in.at[0], part_send.at[0], part_recv.at[0], (dp, right))
    far_left = send(far_out.at[second_half], far_in.at[1], part_send.at[1], part_recv.at[1], (dp, left))
    partial[0] = sum_messages(0)
    partial[1] = sum_messages(1)
    upper, lower = pl.ds(0, half_atoms), pl.ds(half_atoms, half_atoms)
    cot_left.wait_recv()
    relay_left = send(cot_in.at[0, upper], cot_in.at[1, upper], cot_send.at[2], cot_recv.at[2], (dp, left))
    cot_right.wait_recv()
    relay_right = send(cot_in.at[2, lower], cot_in.at[1, lower], cot_send.at[3], cot_recv.at[3], (dp, right))
    partial[2] = sum_messages(3)
    far_right.wait_recv()
    near_out[0, first_half, :] = (partial[1, first_half, :] + far_in[0].astype(F32)).astype(BF16)
    near_out[0, second_half, :] = partial[1, second_half, :].astype(BF16)
    near_right = send(near_out.at[0], near_in.at[0], part_send.at[2], part_recv.at[2], (dp, right))
    far_left.wait_recv()
    near_out[1, first_half, :] = partial[2, first_half, :].astype(BF16)
    near_out[1, second_half, :] = (partial[2, second_half, :] + far_in[1].astype(F32)).astype(BF16)
    near_left = send(near_out.at[1], near_in.at[1], part_send.at[3], part_recv.at[3], (dp, left))

    edge = backward(0, cot[...], True)
    edge = edge + backward(1, cot_in[0], False)
    edge = edge + backward(3, cot_in[2], False)
    relay_left.wait_recv()
    relay_right.wait_recv()
    edge = edge + backward(2, cot_in[1], False)

    hi, lo = split(acc[...])
    grad_src = mm(normed_t, hi, 1, 1) + mm(normed_t, lo, 1, 1)
    grad_edge = edge.T
    rows = chans // pieces
    for i in range(pieces):
        pack_a[i, 0:rows, :] = grad_src[i * rows:(i + 1) * rows, :]
        pack_a[i, rows:2 * rows, :] = grad_edge[i * rows:(i + 1) * rows, :]
    copies = []
    for k in range(1, pieces):
        target = lax.rem(dp + k, pieces)
        copies.append(send(pack_a.at[target], land_a.at[k - 1], a_send.at[k - 1], a_recv.at[k - 1], (target, me)))

    dnorm = (mm(w_src[...], hi, 1, 0) + mm(w_src[...], lo, 1, 0)).T
    grad_gain = jnp.sum(dnorm * h * inv, axis=0, keepdims=True)
    near_right.wait_recv()
    near_left.wait_recv()
    summed = partial[0] + near_in[0].astype(F32) + near_in[1].astype(F32)
    agg_t = (summed / DEG_NORM).astype(BF16)
    grad_out = mm(agg_t, cot[...], 1, 0)
    gains = jnp.broadcast_to(grad_gain, (rows, chans))
    for i in range(pieces):
        pack_b[i, 0:rows, :] = grad_out[i * rows:(i + 1) * rows, :]
        pack_b[i, rows:2 * rows, :] = gains
    for k in range(1, pieces):
        target = lax.rem(dp + k, pieces)
        copies.append(send(pack_b.at[target], land_b.at[k - 1], b_send.at[k - 1], b_recv.at[k - 1], (target, me)))

    layer_out[...] = (h + mm(agg_t, w_out[...], 0, 0)).astype(BF16)
    scaled = gain[...] * dnorm
    grad_atoms[...] = (
        cot[...].astype(F32) + inv * scaled - h * (inv * inv * inv) * jnp.mean(h * scaled, axis=-1, keepdims=True)
    ).astype(BF16)

    for copy in copies:
        copy.wait_recv()
    total_a, total_b = pack_a[dp], pack_b[dp]
    for k in range(1, pieces):
        total_a = total_a + land_a[k - 1]
        total_b = total_b + land_b[k - 1]
    held[me, 0:2 * rows, :] = total_a
    held[me, 2 * rows:4 * rows, :] = total_b
    swaps = [
        send(held.at[me], held.at[me], s_send.at[k - 1], s_recv.at[k - 1], (dp, peers[k]))
        for k in range(1, shards)
    ]
    for copy in [*copies, *dst_copies, cot_left, cot_right, relay_left, relay_right, far_left, far_right, near_left, near_right]:
        copy.wait_send()
    for copy in swaps:
        copy.wait()
    sums[...] = (held[0] + held[1]) + (held[2] + held[3])


def results_kernel(layer, atoms_grad, sums, layer_out, grad_atoms, out_src, out_edge, out_out, out_gain):
    layer_out[...] = layer[...]
    grad_atoms[...] = atoms_grad[...]
    rows = out_src.shape[0]
    lanes = sums.shape[1]
    out_src[...] = sums[0:rows, :]
    out_edge[...] = sums[rows:2 * rows, :]
    out_out[...] = sums[2 * rows:3 * rows, :]
    gains = jnp.broadcast_to(sums[3 * rows:3 * rows + 1, :], (8, lanes))
    shift = lax.rem(lanes - lax.axis_index("dp") * rows, lanes)
    out_gain[...] = pltpu.roll(gains, shift, 1)[0:1, 0:rows]


def body(dp, shards, atoms, gain, w_src, w_edge, w_out, send_src, recv_dst, edge_count, edge_feat, cotangent):
    atom_count, chans = atoms.shape[2:]
    slots = send_src.shape[3]
    width = w_src.shape[1]
    vmem = pl.BlockSpec(memory_space=pltpu.VMEM)
    smem = pl.BlockSpec(memory_space=pltpu.SMEM)
    shape = jax.ShapeDtypeStruct
    rows = chans // dp
    dma = pltpu.SemaphoreType.DMA
    layer, atoms_grad, sums = pl.pallas_call(
        functools.partial(layer_kernel, dp),
        out_shape=[shape((atom_count, chans), BF16), shape((atom_count, chans), BF16), shape((4 * rows, chans), F32)],
        in_specs=[smem] + [vmem] * 8 + [pl.BlockSpec(memory_space=pl.ANY)],
        out_specs=[vmem] * 3,
        scratch_shapes=[
            pltpu.VMEM((shards - 1, shards, slots), jnp.int32),
            pltpu.VMEM((shards - 1, atom_count, chans), BF16),
            pltpu.VMEM((shards, slots, edge_feat.shape[4]), BF16),
            pltpu.VMEM((shards, width, slots), BF16),
            pltpu.VMEM((shards, width, slots), F32),
            pltpu.VMEM((3, width, atom_count), F32),
            pltpu.VMEM((width, atom_count), BF16),
            pltpu.VMEM((2, width // 2, atom_count), BF16),
            pltpu.VMEM((2, width, atom_count), BF16),
            pltpu.VMEM((2, width, atom_count), BF16),
            pltpu.VMEM((width, atom_count), F32),
            pltpu.VMEM((dp, 2 * rows, chans), F32),
            pltpu.VMEM((dp, 2 * rows, chans), F32),
            pltpu.VMEM((dp - 1, 2 * rows, chans), F32),
            pltpu.VMEM((dp - 1, 2 * rows, chans), F32),
            pltpu.VMEM((shards, 4 * rows, chans), F32),
            dma((shards,)), dma((shards - 1,)), dma((shards - 1,)), dma((4,)), dma((4,)), dma((4,)), dma((4,)),
            dma((dp - 1,)), dma((dp - 1,)), dma((dp - 1,)), dma((dp - 1,)), dma((shards - 1,)), dma((shards - 1,)),
        ],
        compiler_params=pltpu.CompilerParams(collective_id=0, has_side_effects=True, vmem_limit_bytes=VMEM_LIMIT),
        name="layer",
    )(
        edge_count.reshape(shards, shards), atoms.reshape(atom_count, chans), gain.reshape(1, chans), w_src, w_edge, w_out,
        send_src.reshape(shards, slots), recv_dst.reshape(shards, slots), cotangent.reshape(atom_count, chans),
        edge_feat.reshape(shards, slots, edge_feat.shape[4]),
    )
    layer_out, grad_atoms, out_src, out_edge, out_out, out_gain = pl.pallas_call(
        results_kernel,
        out_shape=[shape((atom_count, chans), BF16)] * 2 + [shape((rows, width), F32)] * 3 + [shape((1, rows), F32)],
        in_specs=[vmem] * 3,
        out_specs=[vmem] * 6,
        name="results",
    )(layer, atoms_grad, sums)
    return (layer_out.reshape(atoms.shape), grad_atoms.reshape(atoms.shape), out_src, out_edge, out_out, out_gain.reshape(rows))


def solution(mesh):
    in_specs = (
        P("dp", "graph", None, None),
        P(),
        P(),
        P(),
        P(),
        P("dp", "graph", None, None),
        P("dp", "graph", None, None),
        P("dp", None, None),
        P("dp", "graph", None, None, None),
        P("dp", "graph", None, None),
    )
    out_specs = (
        P("dp", "graph", None, None),
        P("dp", "graph", None, None),
        P("dp", None),
        P("dp", None),
        P("dp", None),
        P("dp"),
    )
    return jax.shard_map(
        functools.partial(body, mesh.shape["dp"], mesh.shape["graph"]),
        mesh=mesh, in_specs=in_specs, out_specs=out_specs, check_vma=False)
```

```python
import functools

import jax
import jax.numpy as jnp
from jax import lax
from jax.experimental import pallas as pl
from jax.experimental.pallas import tpu as pltpu
from jax.sharding import PartitionSpec as P

DEG_NORM = 23.0
LANES = 128
MESH = pl.DeviceIdType.MESH
F32 = jnp.float32
BF16 = jnp.bfloat16
I16 = jnp.int16
VMEM_LIMIT = 56 << 20


def mm(a, b, ca, cb):
    return lax.dot_general(a, b, (((ca,), (cb,)), ((), ())), preferred_element_type=F32)


def split(x):
    hi = x.astype(BF16)
    return hi, (x - hi.astype(F32)).astype(BF16)


def ones_where(mask):
    return jnp.where(mask, jnp.array(1, BF16), jnp.array(0, BF16))


def pick_form(index, atoms):
    rows = lax.broadcasted_iota(jnp.int32, (atoms, index.shape[1]), 0).astype(I16)
    return ones_where(rows == index.astype(I16))


def sum_form(index, atoms):
    column = jnp.concatenate([
        jnp.broadcast_to(index[:, k:k + LANES], (LANES, LANES)).astype(F32).T.astype(jnp.int32).astype(I16)
        for k in range(0, index.shape[1], LANES)
    ], 0)
    return jnp.concatenate([
        ones_where((lax.broadcasted_iota(jnp.int32, column.shape, 1) + a).astype(I16) == column)
        for a in range(0, atoms, LANES)
    ], 1)


def layer_kernel(pieces, counts, atoms, gain, w_src, w_edge, w_out, src, dst, cot, feat_hbm,
                 layer_out, grad_atoms, sums,
                 dst_rows, dst_in, cot_in, feat, msg, slope, partial, far_out, far_in, near_out, near_in, acc,
                 pack_a, pack_b, land_a, land_b, held,
                 feat_sem, dst_send, dst_recv, cot_send, cot_recv, part_send, part_recv,
                 a_send, a_recv, b_send, b_recv, s_send, s_recv):
    dp = lax.axis_index("dp")
    me = lax.axis_index("graph")
    shards = 4
    atom_count, chans = atoms.shape
    slots = src.shape[1]
    half_atoms, half_rows = atom_count // 2, acc.shape[0] // 2
    right, left = lax.rem(me + 1, shards), lax.rem(me + shards - 1, shards)

    barrier = pltpu.get_barrier_semaphore()
    for k in range(1, shards):
        pl.semaphore_signal(barrier, inc=1, device_id=(dp, lax.rem(me + k, shards)), device_id_type=MESH)
    for k in range(1, pieces):
        pl.semaphore_signal(barrier, inc=1, device_id=(lax.rem(dp + k, pieces), me), device_id_type=MESH)

    def send(source, target, send_sem, recv_sem, device):
        copy = pltpu.make_async_remote_copy(
            src_ref=source, dst_ref=target, send_sem=send_sem, recv_sem=recv_sem, device_id=device, device_id_type=MESH)
        copy.start()
        return copy

    peers = [lax.rem(me + j, shards) for j in range(shards)]
    loads = [pltpu.make_async_copy(feat_hbm.at[peers[j]], feat.at[j], feat_sem.at[j]) for j in range(shards)]
    for j in (0, 2, 1, 3):
        loads[j].start()

    h = atoms[...].astype(F32)
    inv = lax.rsqrt(jnp.mean(h * h, axis=-1, keepdims=True) + 1e-06)
    normed_t = (h * inv * gain[...]).astype(BF16).T
    w_src_t = w_src[...].T
    w_edge_t = w_edge[...].T
    for k in range(shards):
        dst_rows[k] = dst[k:k + 1, :]

    def forward(j):
        loads[j].wait()
        rows_t = mm(normed_t, pick_form(src[pl.ds(peers[j], 1), :], atom_count), 1, 0).astype(BF16)
        pre = mm(w_src_t, rows_t, 1, 0) + mm(w_edge_t, feat[j], 1, 1)
        sig = 0.5 * jnp.tanh(0.5 * pre) + 0.5
        slot = lax.broadcasted_iota(jnp.int32, pre.shape, 1)
        sig = jnp.where(slot < counts[me, peers[j]], sig, 0.0)
        msg[j] = (pre * sig).astype(BF16)
        slope[j] = sig * (1.0 + pre * (1.0 - sig))

    def targets(j):
        return dst[pl.ds(me, 1), :] if j == 0 else dst_in[j - 1]

    def sum_messages(j):
        return mm(msg[j], sum_form(targets(j), atom_count), 1, 0)

    def backward(j, cot_j):
        back = (mm(w_out[...], cot_j, 1, 1) / DEG_NORM).astype(BF16)
        slot_back = mm(back, pick_form(targets(j), atom_count), 1, 0)
        dpre = (slot_back * slope[j]).astype(BF16)
        total = mm(dpre, sum_form(src[pl.ds(peers[j], 1), :], atom_count), 1, 0)
        acc[...] = total if j == 0 else acc[...] + total
        return mm(dpre, feat[j], 1, 0)

    forward(0)
    pl.semaphore_wait(barrier, pieces + shards - 2)
    dst_copies = []
    for k in (2, 1, 3):
        slot = shards - k - 1
        dst_copies.append(send(dst_rows.at[peers[k]], dst_in.at[slot], dst_send.at[slot], dst_recv.at[slot], (dp, peers[k])))
    upper, lower = pl.ds(0, half_atoms), pl.ds(half_atoms, half_atoms)
    cot_left = [
        send(cot.at[part], cot_in.at[0, part], cot_send.at[n], cot_recv.at[n], (dp, left)) for n, part in ((0, upper), (1, lower))
    ]
    cot_right = [
        send(cot.at[part], cot_in.at[2, part], cot_send.at[n], cot_recv.at[n], (dp, right)) for n, part in ((2, lower), (3, upper))
    ]
    for j in (2, 1, 3):
        forward(j)
    for copy in dst_copies:
        copy.wait_recv()

    far_out[...] = sum_messages(2).astype(BF16)
    first_half, second_half = pl.ds(0, half_rows), pl.ds(half_rows, half_rows)
    far_right = send(far_out.at[first_half], far_in.at[0], part_send.at[0], part_recv.at[0], (dp, right))
    far_left = send(far_out.at[second_half], far_in.at[1], part_send.at[1], part_recv.at[1], (dp, left))
    partial[1] = sum_messages(1)
    partial[2] = sum_messages(3)
    partial[0] = sum_messages(0)
    edge = backward(0, cot[...])
    cot_left[0].wait_recv()
    relay_left = send(cot_in.at[0, upper], cot_in.at[1, upper], cot_send.at[4], cot_recv.at[4], (dp, left))
    cot_right[0].wait_recv()
    relay_right = send(cot_in.at[2, lower], cot_in.at[1, lower], cot_send.at[5], cot_recv.at[5], (dp, right))
    far_right.wait_recv()
    near_out[0, first_half, :] = (partial[1, first_half, :] + far_in[0].astype(F32)).astype(BF16)
    near_out[0, second_half, :] = partial[1, second_half, :].astype(BF16)
    near_right = send(near_out.at[0], near_in.at[0], part_send.at[2], part_recv.at[2], (dp, right))
    far_left.wait_recv()
    near_out[1, first_half, :] = partial[2, first_half, :].astype(BF16)
    near_out[1, second_half, :] = (partial[2, second_half, :] + far_in[1].astype(F32)).astype(BF16)
    near_left = send(near_out.at[1], near_in.at[1], part_send.at[3], part_recv.at[3], (dp, left))

    cot_left[1].wait_recv()
    edge = edge + backward(1, cot_in[0])
    cot_right[1].wait_recv()
    edge = edge + backward(3, cot_in[2])
    relay_left.wait_recv()
    relay_right.wait_recv()
    grad_out = (
        mm(partial[0].astype(BF16), cot[...], 1, 0) + mm(partial[1].astype(BF16), cot_in[0], 1, 0)
        + mm(far_out[...], cot_in[1], 1, 0) + mm(partial[2].astype(BF16), cot_in[2], 1, 0)
    ) / DEG_NORM
    rows = chans // pieces
    copies = []
    for i in range(pieces):
        pack_b[i] = grad_out[i * rows:(i + 1) * rows, :]
    for k in range(1, pieces):
        target = lax.rem(dp + k, pieces)
        copies.append(send(pack_b.at[target], land_b.at[k - 1], b_send.at[k - 1], b_recv.at[k - 1], (target, me)))
    edge = edge + backward(2, cot_in[1])

    hi, lo = split(acc[...])
    grad_src = mm(normed_t, hi, 1, 1) + mm(normed_t, lo, 1, 1)
    grad_edge = edge.T
    for i in range(pieces):
        pack_a[i, 0:rows, :] = grad_src[i * rows:(i + 1) * rows, :]
        pack_a[i, rows:2 * rows, :] = grad_edge[i * rows:(i + 1) * rows, :]
    for k in range(1, pieces):
        target = lax.rem(dp + k, pieces)
        copies.append(send(pack_a.at[target], land_a.at[k - 1], a_send.at[k - 1], a_recv.at[k - 1], (target, me)))

    dnorm = (mm(w_src[...], hi, 1, 0) + mm(w_src[...], lo, 1, 0)).T
    scaled = gain[...] * dnorm
    grad_atoms[...] = (
        cot[...].astype(F32) + inv * scaled - h * (inv * inv * inv) * jnp.mean(h * scaled, axis=-1, keepdims=True)
    ).astype(BF16)
    near_right.wait_recv()
    near_left.wait_recv()
    summed = partial[0] + near_in[0].astype(F32) + near_in[1].astype(F32)
    layer_out[...] = (h + mm((summed / DEG_NORM).astype(BF16), w_out[...], 0, 0)).astype(BF16)

    for copy in copies:
        copy.wait_recv()
    total_a, total_b = pack_a[dp], pack_b[dp]
    for k in range(1, pieces):
        total_a = total_a + land_a[k - 1]
        total_b = total_b + land_b[k - 1]
    held[me, 0:2 * rows, :] = total_a
    held[me, 2 * rows:3 * rows, :] = total_b
    swaps = [
        send(held.at[me], held.at[me], s_send.at[k - 1], s_recv.at[k - 1], (dp, peers[k]))
        for k in range(1, shards)
    ]
    for copy in [*copies, *dst_copies, *cot_left, *cot_right, relay_left, relay_right, far_left, far_right, near_left, near_right]:
        copy.wait_send()
    for copy in swaps:
        copy.wait()
    sums[...] = (held[0] + held[1]) + (held[2] + held[3])


def results_kernel(gain, w_src, layer, atoms_grad, sums, layer_out, grad_atoms, out_src, out_edge, out_out, out_gain):
    layer_out[...] = layer[...]
    grad_atoms[...] = atoms_grad[...]
    rows, lanes = out_src.shape
    first = lax.axis_index("dp") * rows
    grad_src = sums[0:rows, :]
    out_src[...] = grad_src
    out_edge[...] = sums[rows:2 * rows, :]
    out_out[...] = sums[2 * rows:3 * rows, :]
    row = lax.broadcasted_iota(jnp.int32, (rows, lanes), 0)
    lane = lax.broadcasted_iota(jnp.int32, (rows, lanes), 1)
    mine = mm(ones_where(lane == row + first), w_src[...], 1, 0)
    weighted = jnp.sum(mine * grad_src, axis=1, keepdims=True)
    spread = jnp.sum(jnp.where(lane == row, weighted, 0.0), axis=0, keepdims=True)
    gains = pltpu.roll(jnp.broadcast_to(gain[...], (8, lanes)), lax.rem(lanes - first, lanes), 1)
    out_gain[...] = spread[:, 0:rows] / gains[0:1, 0:rows]


def body(dp, shards, atoms, gain, w_src, w_edge, w_out, send_src, recv_dst, edge_count, edge_feat, cotangent):
    atom_count, chans = atoms.shape[2:]
    slots = send_src.shape[3]
    width = w_src.shape[1]
    vmem = pl.BlockSpec(memory_space=pltpu.VMEM)
    smem = pl.BlockSpec(memory_space=pltpu.SMEM)
    shape = jax.ShapeDtypeStruct
    rows = chans // dp
    dma = pltpu.SemaphoreType.DMA
    layer, atoms_grad, sums = pl.pallas_call(
        functools.partial(layer_kernel, dp),
        out_shape=[shape((atom_count, chans), BF16), shape((atom_count, chans), BF16), shape((3 * rows, chans), F32)],
        in_specs=[smem] + [vmem] * 8 + [pl.BlockSpec(memory_space=pl.ANY)],
        out_specs=[vmem] * 3,
        scratch_shapes=[
            pltpu.VMEM((shards, 1, slots), jnp.int32),
            pltpu.VMEM((shards - 1, 1, slots), jnp.int32),
            pltpu.VMEM((shards - 1, atom_count, chans), BF16),
            pltpu.VMEM((shards, slots, edge_feat.shape[4]), BF16),
            pltpu.VMEM((shards, width, slots), BF16),
            pltpu.VMEM((shards, width, slots), F32),
            pltpu.VMEM((3, width, atom_count), F32),
            pltpu.VMEM((width, atom_count), BF16),
            pltpu.VMEM((2, width // 2, atom_count), BF16),
            pltpu.VMEM((2, width, atom_count), BF16),
            pltpu.VMEM((2, width, atom_count), BF16),
            pltpu.VMEM((width, atom_count), F32),
            pltpu.VMEM((dp, 2 * rows, chans), F32),
            pltpu.VMEM((dp, rows, chans), F32),
            pltpu.VMEM((dp - 1, 2 * rows, chans), F32),
            pltpu.VMEM((dp - 1, rows, chans), F32),
            pltpu.VMEM((shards, 3 * rows, chans), F32),
            dma((shards,)), dma((shards - 1,)), dma((shards - 1,)), dma((6,)), dma((6,)), dma((4,)), dma((4,)),
            dma((dp - 1,)), dma((dp - 1,)), dma((dp - 1,)), dma((dp - 1,)), dma((shards - 1,)), dma((shards - 1,)),
        ],
        compiler_params=pltpu.CompilerParams(collective_id=0, has_side_effects=True, vmem_limit_bytes=VMEM_LIMIT),
        name="layer",
    )(
        edge_count.reshape(shards, shards), atoms.reshape(atom_count, chans), gain.reshape(1, chans), w_src, w_edge, w_out,
        send_src.reshape(shards, slots), recv_dst.reshape(shards, slots), cotangent.reshape(atom_count, chans),
        edge_feat.reshape(shards, slots, edge_feat.shape[4]),
    )
    layer_out, grad_atoms, out_src, out_edge, out_out, out_gain = pl.pallas_call(
        results_kernel,
        out_shape=[shape((atom_count, chans), BF16)] * 2 + [shape((rows, width), F32)] * 3 + [shape((1, rows), F32)],
        in_specs=[vmem] * 5,
        out_specs=[vmem] * 6,
        name="results",
    )(gain.reshape(1, chans), w_src, layer, atoms_grad, sums)
    return (layer_out.reshape(atoms.shape), grad_atoms.reshape(atoms.shape), out_src, out_edge, out_out, out_gain.reshape(rows))


def solution(mesh):
    in_specs = (
        P("dp", "graph", None, None),
        P(),
        P(),
        P(),
        P(),
        P("dp", "graph", None, None),
        P("dp", "graph", None, None),
        P("dp", None, None),
        P("dp", "graph", None, None, None),
        P("dp", "graph", None, None),
    )
    out_specs = (
        P("dp", "graph", None, None),
        P("dp", "graph", None, None),
        P("dp", None),
        P("dp", None),
        P("dp", None),
        P("dp"),
    )
    return jax.shard_map(
        functools.partial(body, mesh.shape["dp"], mesh.shape["graph"]),
        mesh=mesh, in_specs=in_specs, out_specs=out_specs, check_vma=False)
```

```python
import functools

import jax
import jax.numpy as jnp
from jax import lax
from jax.experimental import pallas as pl
from jax.experimental.pallas import tpu as pltpu
from jax.sharding import PartitionSpec as P

DEG_NORM = 23.0
LANES = 128
MESH = pl.DeviceIdType.MESH
F32 = jnp.float32
BF16 = jnp.bfloat16
I16 = jnp.int16
VMEM_LIMIT = 56 << 20


def mm(a, b, ca, cb):
    return lax.dot_general(a, b, (((ca,), (cb,)), ((), ())), preferred_element_type=F32)


def split(x):
    hi = x.astype(BF16)
    return hi, (x - hi.astype(F32)).astype(BF16)


def ones_where(mask):
    return jnp.where(mask, jnp.array(1, BF16), jnp.array(0, BF16))


def pick_form(index, atoms):
    rows = lax.broadcasted_iota(jnp.int32, (atoms, index.shape[1]), 0).astype(I16)
    return ones_where(rows == index.astype(I16))


def sum_form(index, atoms):
    column = jnp.concatenate([
        jnp.broadcast_to(index[:, k:k + LANES], (LANES, LANES)).astype(F32).T.astype(jnp.int32).astype(I16)
        for k in range(0, index.shape[1], LANES)
    ], 0)
    return jnp.concatenate([
        ones_where((lax.broadcasted_iota(jnp.int32, column.shape, 1) + a).astype(I16) == column)
        for a in range(0, atoms, LANES)
    ], 1)


def layer_kernel(pieces, counts, atoms, gain, w_src, w_edge, w_out, src, dst, cot, feat_hbm,
                 layer_out, grad_atoms, sums,
                 dst_rows, dst_in, cot_in, feat, msg, slope, partial, far_out, far_in, near_out, near_in, acc,
                 pack_a, pack_b, land_a, land_b, held,
                 feat_sem, dst_send, dst_recv, cot_send, cot_recv, part_send, part_recv,
                 a_send, a_recv, b_send, b_recv, s_send, s_recv, ready_y, ready_core):
    dp = lax.axis_index("dp")
    me = lax.axis_index("graph")
    shards = 4
    atom_count, chans = atoms.shape
    slots = src.shape[1]
    half_atoms, half_rows = atom_count // 2, acc.shape[0] // 2
    right, left = lax.rem(me + 1, shards), lax.rem(me + shards - 1, shards)

    barrier = pltpu.get_barrier_semaphore()
    for k in range(1, shards):
        pl.semaphore_signal(barrier, inc=1, device_id=(dp, lax.rem(me + k, shards)), device_id_type=MESH)
    ring = pieces // 2
    side = 4
    core, row, plane = lax.rem(dp, 2), lax.rem(dp // 2, side), dp // (2 * side)
    other = dp + 1 - 2 * core
    along_y = [dp + 2 * (lax.rem(row + k, side) - row) for k in range(1, side)]
    along_z = [dp + 2 * side * (lax.rem(plane + k, ring // side) - plane) for k in range(1, ring // side)]
    for peer in (other, *along_y, *along_z):
        pl.semaphore_signal(barrier, inc=1, device_id=(peer, me), device_id_type=MESH)

    def send(source, target, send_sem, recv_sem, device):
        copy = pltpu.make_async_remote_copy(
            src_ref=source, dst_ref=target, send_sem=send_sem, recv_sem=recv_sem, device_id=device, device_id_type=MESH)
        copy.start()
        return copy

    peers = [lax.rem(me + j, shards) for j in range(shards)]
    loads = [pltpu.make_async_copy(feat_hbm.at[peers[j]], feat.at[j], feat_sem.at[j]) for j in range(shards)]
    for j in (2, 1, 3, 0):
        loads[j].start()

    h = atoms[...].astype(F32)
    inv = lax.rsqrt(jnp.mean(h * h, axis=-1, keepdims=True) + 1e-06)
    normed_t = (h * inv * gain[...]).astype(BF16).T
    w_src_t = w_src[...].T
    w_edge_t = w_edge[...].T
    for k in range(shards):
        dst_rows[k] = dst[k:k + 1, :]

    def forward(j):
        loads[j].wait()
        rows_t = mm(normed_t, pick_form(src[pl.ds(peers[j], 1), :], atom_count), 1, 0).astype(BF16)
        pre = mm(w_src_t, rows_t, 1, 0) + mm(w_edge_t, feat[j], 1, 1)
        sig = 0.5 * jnp.tanh(0.5 * pre) + 0.5
        slot = lax.broadcasted_iota(jnp.int32, pre.shape, 1)
        sig = jnp.where(slot < counts[me, peers[j]], sig, 0.0)
        msg[j] = (pre * sig).astype(BF16)
        slope[j] = sig * (1.0 + pre * (1.0 - sig))

    def targets(j):
        return dst[pl.ds(me, 1), :] if j == 0 else dst_in[j - 1]

    def sum_messages(j):
        return mm(msg[j], sum_form(targets(j), atom_count), 1, 0)

    def backward(j, cot_j):
        back = (mm(w_out[...], cot_j, 1, 1) / DEG_NORM).astype(BF16)
        slot_back = mm(back, pick_form(targets(j), atom_count), 1, 0)
        dpre = (slot_back * slope[j]).astype(BF16)
        total = mm(dpre, sum_form(src[pl.ds(peers[j], 1), :], atom_count), 1, 0)
        acc[...] = total if j == 0 else acc[...] + total
        return mm(dpre, feat[j], 1, 0)

    forward(2)
    pl.semaphore_wait(barrier, shards + len(along_y) + len(along_z))
    dst_copies = []
    for k in (2, 1, 3):
        slot = shards - k - 1
        dst_copies.append(send(dst_rows.at[peers[k]], dst_in.at[slot], dst_send.at[slot], dst_recv.at[slot], (dp, peers[k])))
    upper, lower = pl.ds(0, half_atoms), pl.ds(half_atoms, half_atoms)
    cot_left = [send(cot.at[upper], cot_in.at[0, upper], cot_send.at[0], cot_recv.at[0], (dp, left))]
    cot_right = [send(cot.at[lower], cot_in.at[2, lower], cot_send.at[2], cot_recv.at[2], (dp, right))]
    for peer in along_y:
        pl.semaphore_signal(ready_y, inc=1, device_id=(peer, me), device_id_type=MESH)
    forward(1)
    cot_left.append(send(cot.at[lower], cot_in.at[0, lower], cot_send.at[1], cot_recv.at[1], (dp, left)))
    cot_right.append(send(cot.at[upper], cot_in.at[2, upper], cot_send.at[3], cot_recv.at[3], (dp, right)))
    forward(3)
    for copy in dst_copies:
        copy.wait_recv()
    far_out[...] = sum_messages(2).astype(BF16)
    first_half, second_half = pl.ds(0, half_rows), pl.ds(half_rows, half_rows)
    far_right = send(far_out.at[first_half], far_in.at[0], part_send.at[0], part_recv.at[0], (dp, right))
    far_left = send(far_out.at[second_half], far_in.at[1], part_send.at[1], part_recv.at[1], (dp, left))
    pl.semaphore_wait(ready_y, len(along_y))
    pl.semaphore_signal(ready_core, inc=1, device_id=(other, me), device_id_type=MESH)
    partial[1] = sum_messages(1)
    cot_left[0].wait_recv()
    relay_left = send(cot_in.at[0, upper], cot_in.at[1, upper], cot_send.at[4], cot_recv.at[4], (dp, left))
    cot_right[0].wait_recv()
    relay_right = send(cot_in.at[2, lower], cot_in.at[1, lower], cot_send.at[5], cot_recv.at[5], (dp, right))
    partial[2] = sum_messages(3)
    forward(0)
    far_right.wait_recv()
    near_out[0, first_half, :] = (partial[1, first_half, :] + far_in[0].astype(F32)).astype(BF16)
    near_out[0, second_half, :] = partial[1, second_half, :].astype(BF16)
    near_right = send(near_out.at[0], near_in.at[0], part_send.at[2], part_recv.at[2], (dp, right))
    far_left.wait_recv()
    near_out[1, first_half, :] = partial[2, first_half, :].astype(BF16)
    near_out[1, second_half, :] = (partial[2, second_half, :] + far_in[1].astype(F32)).astype(BF16)
    near_left = send(near_out.at[1], near_in.at[1], part_send.at[3], part_recv.at[3], (dp, left))
    partial[0] = sum_messages(0)
    edge = backward(0, cot[...])
    pl.semaphore_wait(ready_core, 1)

    cot_left[1].wait_recv()
    edge = edge + backward(1, cot_in[0])
    cot_right[1].wait_recv()
    edge = edge + backward(3, cot_in[2])
    relay_left.wait_recv()
    relay_right.wait_recv()
    grad_out = (
        mm(partial[0].astype(BF16), cot[...], 1, 0) + mm(partial[1].astype(BF16), cot_in[0], 1, 0)
        + mm(far_out[...], cot_in[1], 1, 0) + mm(partial[2].astype(BF16), cot_in[2], 1, 0)
    ) / DEG_NORM
    rows = chans // pieces
    copies = []
    for i in range(pieces):
        pack_b[i] = grad_out[i * rows:(i + 1) * rows, :]
    for k in range(1, pieces):
        target = lax.rem(dp + k, pieces)
        copies.append(send(pack_b.at[target], land_b.at[k - 1], b_send.at[k - 1], b_recv.at[k - 1], (target, me)))
    edge = edge + backward(2, cot_in[1])

    hi, lo = split(acc[...])
    grad_src = mm(normed_t, hi, 1, 1) + mm(normed_t, lo, 1, 1)
    grad_edge = edge.T
    for i in range(pieces):
        pack_a[i, 0:rows, :] = grad_src[i * rows:(i + 1) * rows, :]
        pack_a[i, rows:2 * rows, :] = grad_edge[i * rows:(i + 1) * rows, :]
    for k in range(1, pieces):
        target = lax.rem(dp + k, pieces)
        copies.append(send(pack_a.at[target], land_a.at[k - 1], a_send.at[k - 1], a_recv.at[k - 1], (target, me)))

    dnorm = (mm(w_src[...], hi, 1, 0) + mm(w_src[...], lo, 1, 0)).T
    scaled = gain[...] * dnorm
    grad_atoms[...] = (
        cot[...].astype(F32) + inv * scaled - h * (inv * inv * inv) * jnp.mean(h * scaled, axis=-1, keepdims=True)
    ).astype(BF16)
    near_right.wait_recv()
    near_left.wait_recv()
    summed = partial[0] + near_in[0].astype(F32) + near_in[1].astype(F32)
    layer_out[...] = (h + mm((summed / DEG_NORM).astype(BF16), w_out[...], 0, 0)).astype(BF16)

    for copy in copies:
        copy.wait_recv()
    total_a, total_b = pack_a[dp], pack_b[dp]
    for k in range(1, pieces):
        total_a = total_a + land_a[k - 1]
        total_b = total_b + land_b[k - 1]
    held[me, 0:2 * rows, :] = total_a
    held[me, 2 * rows:3 * rows, :] = total_b
    swaps = [
        send(held.at[me], held.at[me], s_send.at[k - 1], s_recv.at[k - 1], (dp, peers[k]))
        for k in range(1, shards)
    ]
    for copy in [*copies, *dst_copies, *cot_left, *cot_right, relay_left, relay_right, far_left, far_right, near_left, near_right]:
        copy.wait_send()
    for copy in swaps:
        copy.wait()
    sums[...] = (held[0] + held[1]) + (held[2] + held[3])


def results_kernel(gain, w_src, layer, atoms_grad, sums, layer_out, grad_atoms, out_src, out_edge, out_out, out_gain):
    layer_out[...] = layer[...]
    grad_atoms[...] = atoms_grad[...]
    rows, lanes = out_src.shape
    first = lax.axis_index("dp") * rows
    grad_src = sums[0:rows, :]
    out_src[...] = grad_src
    out_edge[...] = sums[rows:2 * rows, :]
    out_out[...] = sums[2 * rows:3 * rows, :]
    row = lax.broadcasted_iota(jnp.int32, (rows, lanes), 0)
    lane = lax.broadcasted_iota(jnp.int32, (rows, lanes), 1)
    mine = mm(ones_where(lane == row + first), w_src[...], 1, 0)
    weighted = jnp.sum(mine * grad_src, axis=1, keepdims=True)
    spread = jnp.sum(jnp.where(lane == row, weighted, 0.0), axis=0, keepdims=True)
    gains = pltpu.roll(jnp.broadcast_to(gain[...], (8, lanes)), lax.rem(lanes - first, lanes), 1)
    out_gain[...] = spread[:, 0:rows] / gains[0:1, 0:rows]


def body(dp, shards, atoms, gain, w_src, w_edge, w_out, send_src, recv_dst, edge_count, edge_feat, cotangent):
    atom_count, chans = atoms.shape[2:]
    slots = send_src.shape[3]
    width = w_src.shape[1]
    vmem = pl.BlockSpec(memory_space=pltpu.VMEM)
    smem = pl.BlockSpec(memory_space=pltpu.SMEM)
    shape = jax.ShapeDtypeStruct
    rows = chans // dp
    dma = pltpu.SemaphoreType.DMA
    layer, atoms_grad, sums = pl.pallas_call(
        functools.partial(layer_kernel, dp),
        out_shape=[shape((atom_count, chans), BF16), shape((atom_count, chans), BF16), shape((3 * rows, chans), F32)],
        in_specs=[smem] + [vmem] * 8 + [pl.BlockSpec(memory_space=pl.ANY)],
        out_specs=[vmem] * 3,
        scratch_shapes=[
            pltpu.VMEM((shards, 1, slots), jnp.int32),
            pltpu.VMEM((shards - 1, 1, slots), jnp.int32),
            pltpu.VMEM((shards - 1, atom_count, chans), BF16),
            pltpu.VMEM((shards, slots, edge_feat.shape[4]), BF16),
            pltpu.VMEM((shards, width, slots), BF16),
            pltpu.VMEM((shards, width, slots), F32),
            pltpu.VMEM((3, width, atom_count), F32),
            pltpu.VMEM((width, atom_count), BF16),
            pltpu.VMEM((2, width // 2, atom_count), BF16),
            pltpu.VMEM((2, width, atom_count), BF16),
            pltpu.VMEM((2, width, atom_count), BF16),
            pltpu.VMEM((width, atom_count), F32),
            pltpu.VMEM((dp, 2 * rows, chans), F32),
            pltpu.VMEM((dp, rows, chans), F32),
            pltpu.VMEM((dp - 1, 2 * rows, chans), F32),
            pltpu.VMEM((dp - 1, rows, chans), F32),
            pltpu.VMEM((shards, 3 * rows, chans), F32),
            dma((shards,)), dma((shards - 1,)), dma((shards - 1,)), dma((6,)), dma((6,)), dma((4,)), dma((4,)),
            dma((dp - 1,)), dma((dp - 1,)), dma((dp - 1,)), dma((dp - 1,)), dma((shards - 1,)), dma((shards - 1,)),
            pltpu.SemaphoreType.REGULAR, pltpu.SemaphoreType.REGULAR,
        ],
        compiler_params=pltpu.CompilerParams(collective_id=0, has_side_effects=True, vmem_limit_bytes=VMEM_LIMIT),
        name="layer",
    )(
        edge_count.reshape(shards, shards), atoms.reshape(atom_count, chans), gain.reshape(1, chans), w_src, w_edge, w_out,
        send_src.reshape(shards, slots), recv_dst.reshape(shards, slots), cotangent.reshape(atom_count, chans),
        edge_feat.reshape(shards, slots, edge_feat.shape[4]),
    )
    layer_out, grad_atoms, out_src, out_edge, out_out, out_gain = pl.pallas_call(
        results_kernel,
        out_shape=[shape((atom_count, chans), BF16)] * 2 + [shape((rows, width), F32)] * 3 + [shape((1, rows), F32)],
        in_specs=[vmem] * 5,
        out_specs=[vmem] * 6,
        name="results",
    )(gain.reshape(1, chans), w_src, layer, atoms_grad, sums)
    return (layer_out.reshape(atoms.shape), grad_atoms.reshape(atoms.shape), out_src, out_edge, out_out, out_gain.reshape(rows))


def solution(mesh):
    in_specs = (
        P("dp", "graph", None, None),
        P(),
        P(),
        P(),
        P(),
        P("dp", "graph", None, None),
        P("dp", "graph", None, None),
        P("dp", None, None),
        P("dp", "graph", None, None, None),
        P("dp", "graph", None, None),
    )
    out_specs = (
        P("dp", "graph", None, None),
        P("dp", "graph", None, None),
        P("dp", None),
        P("dp", None),
        P("dp", None),
        P("dp"),
    )
    return jax.shard_map(
        functools.partial(body, mesh.shape["dp"], mesh.shape["graph"]),
        mesh=mesh, in_specs=in_specs, out_specs=out_specs, check_vma=False)
```
